32 devices in a mesh: grp: 2 (over x), tok: 8 (over z, y), lay: 2 (over core).
Axes of the slice: x: 2, y: 2, z: 4, core: 2. Of those that a mesh axis runs over, the one named last changes fastest.
Arguments:
- acts: bfloat16 [3072, 16, 128], P(('grp', 'tok'), 'lay'), parts along dimension 0, may hold values from -0.5 to 0.5
- grads: bfloat16 [3072, 16, 128], P(('grp', 'tok'), 'lay'), parts along dimension 0, may hold values from -0.5 to 0.5
- losses: bfloat16 [3072, 128], P(('grp', 'tok')), parts along dimension 0, may hold values from -6 to 6
- sources: int32 [3072], P(('grp', 'tok')), parts along dimension 0, may hold values from 0 to 7
Outputs:
- scores: float32 [3072, 128], P(('grp', 'tok', 'lay')), parts along dimension 0
The draws below stay inside these ranges and needn't reach their ends.
There are 2 independent parts, one for each index of `grp`. The reference program is written for one: setup_inputs(seed, part) draws one part's arguments, and reference() takes and returns one part's arrays. A program takes and returns all parts, laid end to end along the dimension named above; each array names one. Nothing has to cross between parts.
All inputs are finite; a program needn't handle non-finite values.
Results may differ from the reference program's by a relative error of at most 0.011.
Values may be sent and summed in bfloat16 or wider, within the bound.
A program may use at most 128 MiB of HBM per device.

```python
import jax
import jax.numpy as jnp
from jax import lax

K = 128
DOM = 128
LAYERS = 16
SOURCES = 8
TOKENS = 1536


def plant(drawn, rng, least, high):
    spot = [jax.random.randint(jax.random.fold_in(rng, axis), (), 0, length) for axis, length in enumerate(drawn.shape)]
    longest = drawn.shape.index(max(drawn.shape))
    beside = spot[:longest] + [(spot[longest] + 1) % drawn.shape[longest]] + spot[longest + 1:]
    return drawn.at[tuple(spot)].set(least).at[tuple(beside)].set(high)


def levels(rng, extent, pieces, smallest, high):
    def one(position, parts):
        heights = jax.random.uniform(jax.random.fold_in(jax.random.fold_in(rng, 6), position), (parts,), jnp.float32, smallest / len(pieces), high / len(pieces))
        return jnp.repeat(jnp.exp(heights), extent[position] // parts).reshape((-1,) + (1,) * (len(extent) - position - 1))

    level = one(*pieces[0])
    for cut in pieces[1:]:
        level = level * one(*cut)
    return level


def scatter_about(own_key, dims, scale, limit, shards=(), dtype=jnp.bfloat16):
    values = scale * jax.random.normal(own_key, dims, jnp.float32)
    if shards:
        values = values * levels(own_key, dims, shards, -0.22, 0.18)
    return jnp.clip(values, -limit, limit).astype(dtype)


def setup_inputs(seed: int = 0, part: int = 0) -> dict:
    arg_keys = jax.random.split(jax.random.key(seed), 5)
    own_keys = jax.random.split(jax.random.fold_in(arg_keys[4], part), 5)
    return {
        "acts": scatter_about(own_keys[0], (TOKENS, LAYERS, K), (K ** -0.5), 0.5, ((0, 8), (1, 2))),
        "grads": scatter_about(own_keys[1], (TOKENS, LAYERS, K), (K ** -0.5), 0.5, ((0, 8), (1, 2))),
        "losses": scatter_about(own_keys[2], (TOKENS, DOM), 1.0, 6.0, ((0, 8),)),
        "sources": plant(jax.random.randint(own_keys[3], (TOKENS,), 0, SOURCES), jax.random.fold_in(own_keys[3], 1), 0, SOURCES - 1).astype(jnp.int32),
    }


def reference(acts, grads, losses, sources):
    influence = jnp.zeros((TOKENS, TOKENS), jnp.float32)
    for layer in range(LAYERS):
        act_layer = acts[:, layer, :].astype(jnp.float32)
        grad_layer = grads[:, layer, :].astype(jnp.float32)
        gram_act = jnp.dot(act_layer, act_layer.T, precision=lax.Precision.HIGHEST)
        gram_grad = jnp.dot(grad_layer, grad_layer.T, precision=lax.Precision.HIGHEST)
        influence = influence + gram_act * gram_grad
    keep = sources[:, None] != sources[None, :]
    masked = jnp.where(keep, influence, jnp.zeros_like(influence)).astype(jnp.bfloat16)
    scale = 1.0 / jnp.sqrt(jnp.float32(TOKENS * LAYERS))
    return jnp.dot(masked, losses, preferred_element_type=jnp.float32) * scale
```

```python
import functools
import math

import jax
import jax.numpy as jnp
from jax import lax
from jax.experimental import pallas as pl
from jax.experimental.pallas import tpu as pltpu
from jax.sharding import PartitionSpec as P

MESH = pl.DeviceIdType.MESH
F32 = jnp.float32
BF16 = jnp.bfloat16
GROUP = 2


def nt(a, b):
    return lax.dot_general(a, b, (((1,), (1,)), ((), ())), preferred_element_type=F32)


def kernel(
    n, lh, scale,
    acts, grads, losses, sources, out,
    fetched, stage, send, recv, lall, srcs, total, xsend, xrecv, rsend, rrecv,
    send_sem, recv_sem, ls_sem, lr_sem, lf_sem, lx_sem, ly_sem, ss_sem, sr_sem,
    xs_sem, xr_sem, rs_sem, rr_sem, in_sem,
):
    block = acts.shape[0]
    half = block // 2
    sets = n // lh
    me = lax.axis_index("tok")
    h = lax.axis_index("lay")
    q, j = me // lh, lax.rem(me, lh)

    def dest(k):
        return lax.rem(q + sets - k // lh, sets) * lh + jnp.bitwise_xor(j, k % lh)

    mine = pl.ds(pl.multiple_of(h * half, half), half)
    theirs = pl.ds(pl.multiple_of((1 - h) * half, half), half)
    peers = list(range(1, n))
    order = sorted(range(1, lh), key=lambda k: (-(k.bit_length()), k))
    send_order = [kq * lh + kj for kj in order for kq in range(sets)] + [kq * lh for kq in range(1, sets)]

    barrier = pltpu.get_barrier_semaphore()
    for k in peers:
        pl.semaphore_signal(barrier, inc=1, device_id={"tok": dest(k)}, device_id_type=MESH)
    pl.semaphore_signal(barrier, inc=1, device_id={"lay": 1 - h}, device_id_type=MESH)

    local = [
        pltpu.make_async_copy(src, dst, in_sem.at[i])
        for i, (src, dst) in enumerate(
            ((acts, fetched.at[0]), (grads, fetched.at[1]), (losses, lall.at[0]), (sources, srcs.at[0]))
        )
    ]
    for copy in local:
        copy.start()

    def cut(kj):
        layer = jnp.bitwise_xor(j, kj)
        for w in range(2):
            piece = stage[w, pl.ds(layer, block, stride=lh), :].astype(BF16)
            if kj == 0:
                recv[0, w] = piece
            if kj or sets > 1:
                send[kj, w] = piece

    ready = order[: lh // 2]
    for w in range(2):
        local[w].wait()
        stage[w] = fetched[w].astype(F32).reshape(block * lh, acts.shape[2])
    for kj in ready:
        cut(kj)
    for copy in local[2:]:
        copy.wait()
    pl.semaphore_wait(barrier, n)

    def remote(src, dst, s, r, **where):
        return pltpu.make_async_remote_copy(
            src_ref=src, dst_ref=dst, send_sem=s, recv_sem=r, device_id=where, device_id_type=MESH
        )

    copies = []

    def go(copy):
        copy.start()
        copies.append(copy)
        return copy

    first = {}
    for k in send_order:
        if k % 2 == 0:
            first[k] = go(remote(lall.at[0, mine], lall.at[k, mine], ls_sem.at[k], lr_sem.at[k], tok=dest(k)))
    first[1] = go(remote(lall.at[0, mine], lall.at[1, mine], ls_sem.at[1], lr_sem.at[1], tok=dest(1)))
    ids = {}
    for k in send_order:
        ids[k] = go(remote(srcs.at[0], srcs.at[k], ss_sem.at[k], sr_sem.at[k], tok=dest(k)))
    main = {}
    for kj in order + [0]:
        if kj not in ready:
            cut(kj)
        for kq in range(sets):
            k = kq * lh + kj
            if k:
                main[k] = go(remote(send.at[kj], recv.at[k], send_sem.at[k], recv_sem.at[k], tok=dest(k)))

    cross = {}
    for k in range(1, n):
        if k % 2 == 0:
            first[k].wait_recv()
            first[k + 1] = go(
                remote(lall.at[k, mine], lall.at[k + 1, mine], lf_sem.at[k + 1], lr_sem.at[k + 1], tok=dest(1))
            )
            cross[k] = go(remote(lall.at[k, mine], lall.at[k, mine], lx_sem.at[k], ly_sem.at[k], lay=1 - h))
    for k in range(1, n):
        if k % 2 == 1:
            first[k].wait_recv()
            cross[k] = go(remote(lall.at[k, mine], lall.at[k, mine], lx_sem.at[k], ly_sem.at[k], lay=1 - h))

    size = GROUP * block
    flat = (size, acts.shape[2])

    def part(ref_slice):
        return ref_slice.reshape(flat)

    def arrive(g):
        for k in range(g * GROUP, (g + 1) * GROUP):
            if k:
                main[k].wait_recv()
                ids[k].wait_recv()
                cross[k].wait_recv()

    def row_ids(g):
        return jnp.concatenate([srcs[g * GROUP + i] for i in range(GROUP)], axis=1)

    rows = {}
    cols = {}

    def one(a, b, both=False):
        sa, sb = pl.ds(a * GROUP, GROUP), pl.ds(b * GROUP, GROUP)
        x = nt(part(recv[sa, 0]), part(recv[sb, 0])) * nt(part(recv[sa, 1]), part(recv[sb, 1]))
        col = cols[a]
        reps = size // col.shape[1]
        keep = jnp.concatenate([col] * reps, axis=1) != rows[b]
        x = jnp.where(keep, x, 0.0).astype(BF16)
        y = jnp.dot(x, lall[sb].reshape(size, losses.shape[1]), preferred_element_type=F32)
        if not both:
            return y
        z = lax.dot_general(x, lall[sa].reshape(size, losses.shape[1]), (((0,), (0,)), ((), ())), preferred_element_type=F32)
        return y, z

    dom = losses.shape[1]

    def add(a, b):
        total[pl.ds(a * GROUP, GROUP)] += one(a, b).reshape(GROUP, block, dom)

    def full(g, after=None):
        acc = one(g, g)
        for a in sorted(range(g), key=lambda a: (-(a.bit_length()), a)):
            y, z = one(a, g, True)
            total[pl.ds(a * GROUP, GROUP)] += y.reshape(GROUP, block, dom)
            acc = acc + z
            if after and a == g - 1:
                after(a)
        total[pl.ds(g * GROUP, GROUP)] = acc.reshape(GROUP, block, dom)

    swaps = {}
    back = {}

    def swap(a):
        at = pl.ds(a * GROUP, GROUP)
        xsend[at] = total[at, theirs].astype(BF16)
        swaps[a] = go(remote(xsend.at[at], xrecv.at[at], xs_sem.at[a], xr_sem.at[a], lay=1 - h))

    def owners(a):
        swaps[a].wait_recv()
        for k in range(a * GROUP, (a + 1) * GROUP):
            if k:
                rsend[k] = (total[k, mine] + xrecv[k].astype(F32)).astype(BF16)
                back[k] = go(remote(rsend.at[k], rrecv.at[k], rs_sem.at[k], rr_sem.at[k], tok=dest(k)))

    groups = lh // GROUP
    last = groups - 1
    for g in range(groups):
        arrive(g)
        rows[g] = row_ids(g)
        cols[g] = jnp.broadcast_to(rows[g], (128, size)).T
        if g == last and sets == 1:
            break
        full(g)
    if sets > 1:
        for g in range(groups, n // GROUP):
            arrive(g)

        @pl.loop(groups, n // GROUP)
        def _(g):
            there = jnp.concatenate([srcs[g * GROUP + i] for i in range(GROUP)], axis=1)
            sb = pl.ds(g * GROUP, GROUP)
            for a in range(groups):
                sa = pl.ds(a * GROUP, GROUP)
                x = nt(part(recv[sa, 0]), part(recv[sb, 0])) * nt(part(recv[sa, 1]), part(recv[sb, 1]))
                col = jnp.broadcast_to(row_ids(a), (128, size)).T
                keep = jnp.concatenate([col] * (size // 128), axis=1) != there
                x = jnp.where(keep, x, 0.0).astype(BF16)
                y = jnp.dot(x, lall[sb].reshape(size, dom), preferred_element_type=F32)
                total[sa] += y.reshape(GROUP, block, dom)

    turn = sorted(range(groups), key=lambda a: (-(a.bit_length()), a))
    for i, a in enumerate(turn):
        if i == 0 and sets == 1:
            full(last, swap)
            for a in turn[1:]:
                swap(a)
        elif sets > 1:
            swap(a)
    for a in turn:
        owners(a)
    acc = total[0, mine] + xrecv[0].astype(F32)
    for k in order[::-1]:
        back[k].wait_recv()
        acc = acc + rrecv[k].astype(F32)
    out[...] = acc * scale
    for copy in copies:
        copy.wait_send()


def on_device(acts, grads, losses, sources):
    block, lh, width = acts.shape
    dom = losses.shape[1]
    n = lax.axis_size("tok")
    layers = lh * lax.axis_size("lay")
    scale = 1.0 / math.sqrt(n * block * layers)
    half = block // 2
    dma = pltpu.SemaphoreType.DMA
    vmem = pl.BlockSpec(memory_space=pltpu.VMEM)
    pairs = n * block * block * lh
    return pl.pallas_call(
        functools.partial(kernel, n, lh, scale),
        out_shape=jax.ShapeDtypeStruct((half, dom), F32),
        in_specs=[pl.BlockSpec(memory_space=pl.ANY)] * 4,
        out_specs=vmem,
        scratch_shapes=[
            pltpu.VMEM((2, block, lh, width), BF16),
            pltpu.VMEM((2, block * lh, width), F32),
            pltpu.VMEM((lh, 2, block, width), BF16),
            pltpu.VMEM((n, 2, block, width), BF16),
            pltpu.VMEM((n, block, dom), BF16),
            pltpu.VMEM((n, 1, block), jnp.int32),
            pltpu.VMEM((lh, block, dom), F32),
            pltpu.VMEM((lh, half, dom), BF16),
            pltpu.VMEM((lh, half, dom), BF16),
            pltpu.VMEM((lh, half, dom), BF16),
            pltpu.VMEM((lh, half, dom), BF16),
            dma((n,)), dma((n,)), dma((n,)), dma((n,)), dma((n,)), dma((n,)), dma((n,)), dma((n,)), dma((n,)),
            dma((lh,)), dma((lh,)), dma((lh,)), dma((lh,)), dma((4,)),
        ],
        compiler_params=pltpu.CompilerParams(
            collective_id=0, has_side_effects=True, vmem_limit_bytes=56 * 1024 * 1024
        ),
        cost_estimate=pl.CostEstimate(
            flops=2 * pairs * (2 * width + dom), bytes_accessed=4 * block * lh * width, transcendentals=0
        ),
    )(acts, grads, losses, sources.reshape(1, block))


LAG = 4


def near_far(
    scale,
    acts, grads, losses, sources, out,
    fetched, stage, send, recv, own, lall, ids, columns, total, xsend, xrecv, rsend, rrecv,
    send_sem, recv_sem, ls_sem, lr_sem, lx_sem, ly_sem, xs_sem, xr_sem, rs_sem, rr_sem, in_sem,
):
    block, lh, width = acts.shape
    dom = losses.shape[1]
    half = block // 2
    n = 8
    me = lax.axis_index("tok")
    h = lax.axis_index("lay")
    upper = me // 4
    odd = lax.rem(me // 2, 2)
    inner = jnp.bitwise_xor(odd, upper)
    outer = 1 - inner
    mine = pl.ds(pl.multiple_of(h * half, half), half)
    theirs = pl.ds(pl.multiple_of((1 - h) * half, half), half)

    def at(k):
        return jnp.bitwise_xor(me, k)

    barrier = pltpu.get_barrier_semaphore()
    for k in range(n - 1, 0, -1):
        pl.semaphore_signal(barrier, inc=1, device_id={"tok": at(k)}, device_id_type=MESH)
    pl.semaphore_signal(barrier, inc=1, device_id={"lay": 1 - h}, device_id_type=MESH)

    local = [
        pltpu.make_async_copy(src, dst, in_sem.at[i])
        for i, (src, dst) in enumerate(
            ((losses, lall.at[0]), (sources, own), (acts, fetched.at[0]), (grads, fetched.at[1]))
        )
    ]
    for copy in local:
        copy.start()

    def remote(src, dst, s, r, **where):
        return pltpu.make_async_remote_copy(
            src_ref=src, dst_ref=dst, send_sem=s, recv_sem=r, device_id=where, device_id_type=MESH
        )

    copies = []

    def go(copy):
        copy.start()
        copies.append(copy)
        return copy

    side = 2 * block
    tail = pl.ds(side, half + 16)

    def cut(i, layer):
        for w in range(2):
            send[i, pl.ds(w * block, block)] = stage[w, pl.ds(layer, block, stride=lh), :].astype(BF16)

    for copy in local[:2]:
        copy.wait()
    row = jnp.concatenate([own[...], jnp.zeros((1, 256 - block), jnp.int32)], axis=1).astype(F32)
    row = jnp.concatenate([jnp.broadcast_to(row[:, :128], (8, 128)), jnp.broadcast_to(row[:, 128:], (8, 128))])
    note = jnp.concatenate([lall[0, mine], row.astype(BF16)])
    for k in range(4):
        send[k, tail] = note

    far = [4 + jnp.bitwise_xor(t, 2 * outer) for t in range(4)]
    for w in range(2):
        local[2 + w].wait()
        stage[w] = fetched[w].astype(F32).reshape(block * lh, width)
    for t in range(4):
        cut(4 + t, at(far[t]))
    pl.semaphore_wait(barrier, n)

    across = 4 + 2 * inner
    body = pl.ds(0, side)

    def mail(i, k, slot, where):
        return remote(send.at[i, where], recv.at[slot, where], send_sem.at[i], recv_sem.at[slot], tok=at(k))

    def note_to(i, k):
        return remote(send.at[0, tail], recv.at[across, tail], ls_sem.at[i], lr_sem.at[across], tok=at(k))

    for i, k in enumerate((4, 6)):
        go(note_to(i, k))
    for t in range(4):
        go(mail(4 + t, far[t], across + t % 2, body))
    for k in range(1, 4):
        cut(k, at(k))
        go(mail(k, k, k, pl.ds(0, side + half + 16)))
    for w in range(2):
        recv[0, pl.ds(w * block, block)] = stage[w, pl.ds(me, block, stride=lh), :].astype(BF16)
    recv[0, tail] = note

    def landed(sem, slot, where):
        remote(recv.at[slot, where], recv.at[slot, where], ls_sem.at[0], sem.at[slot], tok=at(1)).wait_recv()

    for i, slot in enumerate((4, 6)):
        landed(lr_sem, slot, tail)
        go(remote(recv.at[slot, tail], recv.at[slot + 1, tail], ls_sem.at[2 + i], lr_sem.at[slot + 1], tok=at(1)))

    loss_rows = pl.ds(side, half)

    def share(i, first, count):
        slots = pl.ds(first, count)
        go(remote(recv.at[slots, loss_rows], lall.at[slots, mine], lx_sem.at[i], ly_sem.at[i], lay=1 - h))
        lall[slots, mine] = recv[slots, loss_rows]
        for slot in range(first, first + count):
            row = recv[slot, pl.ds(side + half, 16)].astype(F32)
            row = jnp.concatenate([row[0:1], row[8:9, : block - 128]], axis=1)
            ids[slot] = row
            columns[slot] = jnp.broadcast_to(row, (128, block)).T

    def shared(i, first, count):
        slots = pl.ds(first, count)
        remote(recv.at[slots, loss_rows], lall.at[slots, theirs], lx_sem.at[i], ly_sem.at[i], lay=1 - h).wait_recv()

    def arrive(slot):
        if slot > 3:
            landed(recv_sem, slot, body)

    def product(a, na, b, nb, both):
        sa, sb = pl.ds(a, na), pl.ds(b, nb)
        ra, rb = na * block, nb * block
        x = nt(recv[sa, :block].reshape(ra, width), recv[sb, :block].reshape(rb, width))
        x = x * nt(recv[sa, block:side].reshape(ra, width), recv[sb, block:side].reshape(rb, width))
        col = columns[sa].reshape(ra, 128)
        col = jnp.concatenate([col] * -(-rb // 128), axis=1)[:, :rb]
        row = ids[b] if nb == 1 else jnp.concatenate([ids[b + i] for i in range(nb)], axis=1)
        x = jnp.where(col != row, x, 0.0).astype(BF16)
        y = jnp.dot(x, lall[sb].reshape(rb, dom), preferred_element_type=F32)
        if not both:
            return y
        z = lax.dot_general(x, lall[sa].reshape(ra, dom), (((0,), (0,)), ((), ())), preferred_element_type=F32)
        return y, z

    def full(b, nb, before):
        acc = product(b, nb, b, nb, False)
        for a, na in before:
            y, z = product(a, na, b, nb, True)
            total[pl.ds(a, na)] += y.reshape(na, block, dom)
            acc = acc + z
        total[pl.ds(b, nb)] = acc.reshape(nb, block, dom)

    def swap(a):
        xsend[a] = total[a, theirs].astype(BF16)
        go(remote(xsend.at[a], xrecv.at[a], xs_sem.at[a], xr_sem.at[a], lay=1 - h))

    def owner(a):
        remote(xsend.at[a], xrecv.at[a], xs_sem.at[a], xr_sem.at[a], lay=1 - h).wait_recv()

        @pl.when(a != 0)
        def _():
            rsend[a] = (total[a, mine] + xrecv[a].astype(F32)).astype(BF16)
            give(a).start()

    def give(a):
        far = a // 4
        p = lax.rem(a, 2)
        k = jnp.where(far == 1, 4 + p + 2 * jnp.bitwise_xor(lax.rem(a // 2, 2), outer), a)
        to = jnp.where(far == 1, across + p, a)
        return remote(rsend.at[a], rrecv.at[to], rs_sem.at[a], rr_sem.at[to], tok=at(k))

    for slot in (1, 2, 3):
        landed(recv_sem, slot, pl.ds(0, side + half + 16))
    share(0, 1, 3)
    row = recv[0, pl.ds(side + half, 16)].astype(F32)
    row = jnp.concatenate([row[0:1], row[8:9, : block - 128]], axis=1)
    ids[0] = row
    columns[0] = jnp.broadcast_to(row, (128, block)).T
    for slot in (5, 7):
        landed(lr_sem, slot, tail)
    share(1, 4, 4)
    shared(0, 1, 3)
    full(0, 2, [])
    full(2, 2, [(0, 2)])
    shared(1, 4, 4)
    arrive(4)
    arrive(5)
    full(4, 2, [(0, 2), (2, 2)])
    arrive(6)
    full(6, 1, [(0, 2), (2, 2), (4, 2)])
    arrive(7)
    acc = product(7, 1, 7, 1, False)
    y = lax.rem(me, 2)
    inside = [jnp.bitwise_xor(lax.rem(me, 4), t) for t in range(4)]
    turn = [
        jnp.where(upper == 1, b, a)
        for a, b in zip(inside + [4, 5, 6], [4 + y, 5 - y, 6] + inside)
    ]
    for t, a in enumerate(turn):
        y, z = product(a, 1, 7, 1, True)
        total[a] += y
        acc = acc + z
        swap(a)
        if t >= LAG:
            owner(turn[t - LAG])
    total[7] = acc
    swap(7)
    for a in turn[7 - LAG:]:
        owner(a)
    owner(7)
    acc = total[0, mine] + xrecv[0].astype(F32)
    for a in range(1, n):
        remote(rsend.at[a], rrecv.at[a], rs_sem.at[a], rr_sem.at[a], tok=at(1)).wait_recv()
        acc = acc + rrecv[a].astype(F32)
    out[...] = acc * scale
    for a in range(1, n):
        give(a).wait_send()
    for copy in copies:
        copy.wait_send()


def on_device_near_far(acts, grads, losses, sources):
    block, lh, width = acts.shape
    dom = losses.shape[1]
    n = lax.axis_size("tok")
    layers = lh * lax.axis_size("lay")
    scale = 1.0 / math.sqrt(n * block * layers)
    half = block // 2
    dma = pltpu.SemaphoreType.DMA
    pairs = n * block * block * lh
    return pl.pallas_call(
        functools.partial(near_far, scale),
        out_shape=jax.ShapeDtypeStruct((half, dom), F32),
        in_specs=[pl.BlockSpec(memory_space=pl.ANY)] * 4,
        out_specs=pl.BlockSpec(memory_space=pltpu.VMEM),
        scratch_shapes=[
            pltpu.VMEM((2, block, lh, width), BF16),
            pltpu.VMEM((2, block * lh, width), F32),
            pltpu.VMEM((n, 2 * block + half + 16, width), BF16),
            pltpu.VMEM((n, 2 * block + half + 16, width), BF16),
            pltpu.VMEM((1, block), jnp.int32),
            pltpu.VMEM((n, block, dom), BF16),
            pltpu.VMEM((n, 1, block), F32),
            pltpu.VMEM((n, block, 128), F32),
            pltpu.VMEM((n, block, dom), F32),
            pltpu.VMEM((n, half, dom), BF16),
            pltpu.VMEM((n, half, dom), BF16),
            pltpu.VMEM((n, half, dom), BF16),
            pltpu.VMEM((n, half, dom), BF16),
            dma((n,)), dma((n,)), dma((4,)), dma((n,)), dma((2,)), dma((2,)),
            dma((n,)), dma((n,)), dma((n,)), dma((n,)), dma((4,)),
        ],
        compiler_params=pltpu.CompilerParams(
            collective_id=1, has_side_effects=True, vmem_limit_bytes=56 * 1024 * 1024
        ),
        cost_estimate=pl.CostEstimate(
            flops=2 * pairs * (2 * width + dom), bytes_accessed=4 * block * lh * width, transcendentals=0
        ),
    )(acts, grads, losses, sources.reshape(1, block))


def solution(mesh):
    placed = (
        P(("grp", "tok"), "lay", None),
        P(("grp", "tok"), "lay", None),
        P(("grp", "tok"), None),
        P(("grp", "tok")),
    )
    def part(acts, grads, losses, sources):
        paired = acts.shape[1] == mesh.shape["tok"] == 8
        return (on_device_near_far if paired else on_device)(acts, grads, losses, sources)

    return jax.shard_map(
        part,
        mesh=mesh,
        in_specs=placed,
        out_specs=P(("grp", "tok", "lay"), None),
        check_vma=False,
    )
```

```python
import functools
import math

import jax
import jax.numpy as jnp
from jax import lax
from jax.experimental import pallas as pl
from jax.experimental.pallas import tpu as pltpu
from jax.sharding import PartitionSpec as P

MESH = pl.DeviceIdType.MESH
F32 = jnp.float32
BF16 = jnp.bfloat16
GROUP = 2


def nt(a, b):
    return lax.dot_general(a, b, (((1,), (1,)), ((), ())), preferred_element_type=F32)


def kernel(
    n, lh, scale,
    acts, grads, losses, sources, out,
    fetched, stage, send, recv, lall, srcs, total, xsend, xrecv, rsend, rrecv,
    send_sem, recv_sem, ls_sem, lr_sem, lf_sem, lx_sem, ly_sem, ss_sem, sr_sem,
    xs_sem, xr_sem, rs_sem, rr_sem, in_sem,
):
    block = acts.shape[0]
    half = block // 2
    sets = n // lh
    me = lax.axis_index("tok")
    h = lax.axis_index("lay")
    q, j = me // lh, lax.rem(me, lh)

    def dest(k):
        return lax.rem(q + sets - k // lh, sets) * lh + jnp.bitwise_xor(j, k % lh)

    mine = pl.ds(pl.multiple_of(h * half, half), half)
    theirs = pl.ds(pl.multiple_of((1 - h) * half, half), half)
    peers = list(range(1, n))
    order = sorted(range(1, lh), key=lambda k: (-(k.bit_length()), k))
    send_order = [kq * lh + kj for kj in order for kq in range(sets)] + [kq * lh for kq in range(1, sets)]

    barrier = pltpu.get_barrier_semaphore()
    for k in peers:
        pl.semaphore_signal(barrier, inc=1, device_id={"tok": dest(k)}, device_id_type=MESH)
    pl.semaphore_signal(barrier, inc=1, device_id={"lay": 1 - h}, device_id_type=MESH)

    local = [
        pltpu.make_async_copy(src, dst, in_sem.at[i])
        for i, (src, dst) in enumerate(
            ((acts, fetched.at[0]), (grads, fetched.at[1]), (losses, lall.at[0]), (sources, srcs.at[0]))
        )
    ]
    for copy in local:
        copy.start()

    def cut(kj):
        layer = jnp.bitwise_xor(j, kj)
        for w in range(2):
            piece = stage[w, pl.ds(layer, block, stride=lh), :].astype(BF16)
            if kj == 0:
                recv[0, w] = piece
            if kj or sets > 1:
                send[kj, w] = piece

    ready = order[: lh // 2]
    for w in range(2):
        local[w].wait()
        stage[w] = fetched[w].astype(F32).reshape(block * lh, acts.shape[2])
    for kj in ready:
        cut(kj)
    for copy in local[2:]:
        copy.wait()
    pl.semaphore_wait(barrier, n)

    def remote(src, dst, s, r, **where):
        return pltpu.make_async_remote_copy(
            src_ref=src, dst_ref=dst, send_sem=s, recv_sem=r, device_id=where, device_id_type=MESH
        )

    copies = []

    def go(copy):
        copy.start()
        copies.append(copy)
        return copy

    first = {}
    for k in send_order:
        if k % 2 == 0:
            first[k] = go(remote(lall.at[0, mine], lall.at[k, mine], ls_sem.at[k], lr_sem.at[k], tok=dest(k)))
    first[1] = go(remote(lall.at[0, mine], lall.at[1, mine], ls_sem.at[1], lr_sem.at[1], tok=dest(1)))
    ids = {}
    for k in send_order:
        ids[k] = go(remote(srcs.at[0], srcs.at[k], ss_sem.at[k], sr_sem.at[k], tok=dest(k)))
    main = {}
    for kj in order + [0]:
        if kj not in ready:
            cut(kj)
        for kq in range(sets):
            k = kq * lh + kj
            if k:
                main[k] = go(remote(send.at[kj], recv.at[k], send_sem.at[k], recv_sem.at[k], tok=dest(k)))

    cross = {}
    for k in range(1, n):
        if k % 2 == 0:
            first[k].wait_recv()
            first[k + 1] = go(
                remote(lall.at[k, mine], lall.at[k + 1, mine], lf_sem.at[k + 1], lr_sem.at[k + 1], tok=dest(1))
            )
            cross[k] = go(remote(lall.at[k, mine], lall.at[k, mine], lx_sem.at[k], ly_sem.at[k], lay=1 - h))
    for k in range(1, n):
        if k % 2 == 1:
            first[k].wait_recv()
            cross[k] = go(remote(lall.at[k, mine], lall.at[k, mine], lx_sem.at[k], ly_sem.at[k], lay=1 - h))

    size = GROUP * block
    flat = (size, acts.shape[2])

    def part(ref_slice):
        return ref_slice.reshape(flat)

    def arrive(g):
        for k in range(g * GROUP, (g + 1) * GROUP):
            if k:
                main[k].wait_recv()
                ids[k].wait_recv()
                cross[k].wait_recv()

    def row_ids(g):
        return jnp.concatenate([srcs[g * GROUP + i] for i in range(GROUP)], axis=1)

    rows = {}
    cols = {}

    def one(a, b, both=False):
        sa, sb = pl.ds(a * GROUP, GROUP), pl.ds(b * GROUP, GROUP)
        x = nt(part(recv[sa, 0]), part(recv[sb, 0])) * nt(part(recv[sa, 1]), part(recv[sb, 1]))
        col = cols[a]
        reps = size // col.shape[1]
        keep = jnp.concatenate([col] * reps, axis=1) != rows[b]
        x = jnp.where(keep, x, 0.0).astype(BF16)
        y = jnp.dot(x, lall[sb].reshape(size, losses.shape[1]), preferred_element_type=F32)
        if not both:
            return y
        z = lax.dot_general(x, lall[sa].reshape(size, losses.shape[1]), (((0,), (0,)), ((), ())), preferred_element_type=F32)
        return y, z

    dom = losses.shape[1]

    def add(a, b):
        total[pl.ds(a * GROUP, GROUP)] += one(a, b).reshape(GROUP, block, dom)

    def full(g, after=None):
        acc = one(g, g)
        for a in sorted(range(g), key=lambda a: (-(a.bit_length()), a)):
            y, z = one(a, g, True)
            total[pl.ds(a * GROUP, GROUP)] += y.reshape(GROUP, block, dom)
            acc = acc + z
            if after and a == g - 1:
                after(a)
        total[pl.ds(g * GROUP, GROUP)] = acc.reshape(GROUP, block, dom)

    swaps = {}
    back = {}

    def swap(a):
        at = pl.ds(a * GROUP, GROUP)
        xsend[at] = total[at, theirs].astype(BF16)
        swaps[a] = go(remote(xsend.at[at], xrecv.at[at], xs_sem.at[a], xr_sem.at[a], lay=1 - h))

    def owners(a):
        swaps[a].wait_recv()
        for k in range(a * GROUP, (a + 1) * GROUP):
            if k:
                rsend[k] = (total[k, mine] + xrecv[k].astype(F32)).astype(BF16)
                back[k] = go(remote(rsend.at[k], rrecv.at[k], rs_sem.at[k], rr_sem.at[k], tok=dest(k)))

    groups = lh // GROUP
    last = groups - 1
    for g in range(groups):
        arrive(g)
        rows[g] = row_ids(g)
        cols[g] = jnp.broadcast_to(rows[g], (128, size)).T
        if g == last and sets == 1:
            break
        full(g)
    if sets > 1:
        for g in range(groups, n // GROUP):
            arrive(g)

        @pl.loop(groups, n // GROUP)
        def _(g):
            there = jnp.concatenate([srcs[g * GROUP + i] for i in range(GROUP)], axis=1)
            sb = pl.ds(g * GROUP, GROUP)
            for a in range(groups):
                sa = pl.ds(a * GROUP, GROUP)
                x = nt(part(recv[sa, 0]), part(recv[sb, 0])) * nt(part(recv[sa, 1]), part(recv[sb, 1]))
                col = jnp.broadcast_to(row_ids(a), (128, size)).T
                keep = jnp.concatenate([col] * (size // 128), axis=1) != there
                x = jnp.where(keep, x, 0.0).astype(BF16)
                y = jnp.dot(x, lall[sb].reshape(size, dom), preferred_element_type=F32)
                total[sa] += y.reshape(GROUP, block, dom)

    turn = sorted(range(groups), key=lambda a: (-(a.bit_length()), a))
    for i, a in enumerate(turn):
        if i == 0 and sets == 1:
            full(last, swap)
            for a in turn[1:]:
                swap(a)
        elif sets > 1:
            swap(a)
    for a in turn:
        owners(a)
    acc = total[0, mine] + xrecv[0].astype(F32)
    for k in order[::-1]:
        back[k].wait_recv()
        acc = acc + rrecv[k].astype(F32)
    out[...] = acc * scale
    for copy in copies:
        copy.wait_send()


def on_device(acts, grads, losses, sources):
    block, lh, width = acts.shape
    dom = losses.shape[1]
    n = lax.axis_size("tok")
    layers = lh * lax.axis_size("lay")
    scale = 1.0 / math.sqrt(n * block * layers)
    half = block // 2
    dma = pltpu.SemaphoreType.DMA
    vmem = pl.BlockSpec(memory_space=pltpu.VMEM)
    pairs = n * block * block * lh
    return pl.pallas_call(
        functools.partial(kernel, n, lh, scale),
        out_shape=jax.ShapeDtypeStruct((half, dom), F32),
        in_specs=[pl.BlockSpec(memory_space=pl.ANY)] * 4,
        out_specs=vmem,
        scratch_shapes=[
            pltpu.VMEM((2, block, lh, width), BF16),
            pltpu.VMEM((2, block * lh, width), F32),
            pltpu.VMEM((lh, 2, block, width), BF16),
            pltpu.VMEM((n, 2, block, width), BF16),
            pltpu.VMEM((n, block, dom), BF16),
            pltpu.VMEM((n, 1, block), jnp.int32),
            pltpu.VMEM((lh, block, dom), F32),
            pltpu.VMEM((lh, half, dom), BF16),
            pltpu.VMEM((lh, half, dom), BF16),
            pltpu.VMEM((lh, half, dom), BF16),
            pltpu.VMEM((lh, half, dom), BF16),
            dma((n,)), dma((n,)), dma((n,)), dma((n,)), dma((n,)), dma((n,)), dma((n,)), dma((n,)), dma((n,)),
            dma((lh,)), dma((lh,)), dma((lh,)), dma((lh,)), dma((4,)),
        ],
        compiler_params=pltpu.CompilerParams(
            collective_id=0, has_side_effects=True, vmem_limit_bytes=56 * 1024 * 1024
        ),
        cost_estimate=pl.CostEstimate(
            flops=2 * pairs * (2 * width + dom), bytes_accessed=4 * block * lh * width, transcendentals=0
        ),
    )(acts, grads, losses, sources.reshape(1, block))


def near_far(
    scale,
    acts, grads, losses, sources, out,
    fetched, stage, send, recv, own, lall, ids, columns, total, xsend, xrecv, rsend, rrecv,
    send_sem, recv_sem, ls_sem, lr_sem, lx_sem, ly_sem, xs_sem, xr_sem, rs_sem, rr_sem, in_sem,
):
    block, lh, width = acts.shape
    dom = losses.shape[1]
    half = block // 2
    n = 8
    me = lax.axis_index("tok")
    h = lax.axis_index("lay")
    upper = me // 4
    odd = lax.rem(me // 2, 2)
    inner = jnp.bitwise_xor(odd, upper)
    outer = 1 - inner
    mine = pl.ds(pl.multiple_of(h * half, half), half)
    theirs = pl.ds(pl.multiple_of((1 - h) * half, half), half)

    def at(k):
        return jnp.bitwise_xor(me, k)

    barrier = pltpu.get_barrier_semaphore()
    for k in range(n - 1, 0, -1):
        pl.semaphore_signal(barrier, inc=1, device_id={"tok": at(k)}, device_id_type=MESH)
    pl.semaphore_signal(barrier, inc=1, device_id={"lay": 1 - h}, device_id_type=MESH)

    local = [
        pltpu.make_async_copy(src, dst, in_sem.at[i])
        for i, (src, dst) in enumerate(
            ((losses, lall.at[0]), (sources, own), (acts, fetched.at[0]), (grads, fetched.at[1]))
        )
    ]
    for copy in local:
        copy.start()

    def remote(src, dst, s, r, **where):
        return pltpu.make_async_remote_copy(
            src_ref=src, dst_ref=dst, send_sem=s, recv_sem=r, device_id=where, device_id_type=MESH
        )

    copies = []

    def go(copy):
        copy.start()
        copies.append(copy)
        return copy

    side = 2 * block
    tail = pl.ds(side, half + 16)

    def cut(i, layer):
        for w in range(2):
            send[i, pl.ds(w * block, block)] = stage[w, pl.ds(layer, block, stride=lh), :].astype(BF16)

    for copy in local[:2]:
        copy.wait()
    row = jnp.concatenate([own[...], jnp.zeros((1, 256 - block), jnp.int32)], axis=1).astype(F32)
    row = jnp.concatenate([jnp.broadcast_to(row[:, :128], (8, 128)), jnp.broadcast_to(row[:, 128:], (8, 128))])
    note = jnp.concatenate([lall[0, mine], row.astype(BF16)])
    for k in range(4):
        send[k, tail] = note

    far = [4 + t for t in range(4)]
    for w in range(2):
        local[2 + w].wait()
        stage[w] = fetched[w].astype(F32).reshape(block * lh, width)
    for t in range(4):
        cut(4 + t, at(far[t]))
    pl.semaphore_wait(barrier, n)

    across = 4 + 2 * inner
    body = pl.ds(0, side)

    def mail(i, k, slot, where):
        return remote(send.at[i, where], recv.at[slot, where], send_sem.at[i], recv_sem.at[slot], tok=at(k))

    def note_to(i, k):
        return remote(send.at[0, tail], recv.at[across, tail], ls_sem.at[i], lr_sem.at[across], tok=at(k))

    for i, k in enumerate((4, 6)):
        go(note_to(i, k))
    for t in range(4):
        go(mail(4 + t, far[t], across + t % 2, body))
    for k in range(1, 4):
        cut(k, at(k))
        go(mail(k, k, k, pl.ds(0, side + half + 16)))
    for w in range(2):
        recv[0, pl.ds(w * block, block)] = stage[w, pl.ds(me, block, stride=lh), :].astype(BF16)
    recv[0, tail] = note

    def landed(sem, slot, where):
        remote(recv.at[slot, where], recv.at[slot, where], ls_sem.at[0], sem.at[slot], tok=at(1)).wait_recv()

    for i, slot in enumerate((4, 6)):
        landed(lr_sem, slot, tail)
        go(remote(recv.at[slot, tail], recv.at[slot + 1, tail], ls_sem.at[2 + i], lr_sem.at[slot + 1], tok=at(1)))

    loss_rows = pl.ds(side, half)

    def share(i, first, count):
        slots = pl.ds(first, count)
        go(remote(recv.at[slots, loss_rows], lall.at[slots, mine], lx_sem.at[i], ly_sem.at[i], lay=1 - h))
        lall[slots, mine] = recv[slots, loss_rows]
        for slot in range(first, first + count):
            row = recv[slot, pl.ds(side + half, 16)].astype(F32)
            row = jnp.concatenate([row[0:1], row[8:9, : block - 128]], axis=1)
            ids[slot] = row
            columns[slot] = jnp.broadcast_to(row, (128, block)).T

    def shared(i, first, count):
        slots = pl.ds(first, count)
        remote(recv.at[slots, loss_rows], lall.at[slots, theirs], lx_sem.at[i], ly_sem.at[i], lay=1 - h).wait_recv()

    def arrive(slot):
        if slot > 3:
            landed(recv_sem, slot, body)

    def product(a, na, b, nb, both):
        sa, sb = pl.ds(a, na), pl.ds(b, nb)
        ra, rb = na * block, nb * block
        x = nt(recv[sa, :block].reshape(ra, width), recv[sb, :block].reshape(rb, width))
        x = x * nt(recv[sa, block:side].reshape(ra, width), recv[sb, block:side].reshape(rb, width))
        col = columns[sa].reshape(ra, 128)
        col = jnp.concatenate([col] * -(-rb // 128), axis=1)[:, :rb]
        row = ids[b] if nb == 1 else jnp.concatenate([ids[b + i] for i in range(nb)], axis=1)
        x = jnp.where(col != row, x, 0.0).astype(BF16)
        y = jnp.dot(x, lall[sb].reshape(rb, dom), preferred_element_type=F32)
        if not both:
            return y
        z = lax.dot_general(x, lall[sa].reshape(ra, dom), (((0,), (0,)), ((), ())), preferred_element_type=F32)
        return y, z

    def full(b, nb, before):
        acc = product(b, nb, b, nb, False)
        for a, na in before:
            y, z = product(a, na, b, nb, True)
            total[pl.ds(a, na)] += y.reshape(na, block, dom)
            acc = acc + z
        total[pl.ds(b, nb)] = acc.reshape(nb, block, dom)

    def swap(i, first, count):
        slots = pl.ds(first, count)
        return remote(xsend.at[slots], xrecv.at[slots], xs_sem.at[i], xr_sem.at[i], lay=1 - h)

    def offer(i, first, count):
        slots = pl.ds(first, count)
        xsend[slots] = total[slots, theirs].astype(BF16)
        swap(i, first, count).start()

    def owner(a):
        @pl.when(a != 0)
        def _():
            rsend[a] = (total[a, mine] + xrecv[a].astype(F32)).astype(BF16)
            give(a).start()

    def give(a):
        far = a // 4
        p = lax.rem(a, 2)
        k = jnp.where(far == 1, 4 + p + 2 * jnp.bitwise_xor(lax.rem(a // 2, 2), outer), a)
        to = jnp.where(far == 1, across + p, a)
        return remote(rsend.at[a], rrecv.at[to], rs_sem.at[a], rr_sem.at[to], tok=at(k))

    for slot in (1, 2, 3):
        landed(recv_sem, slot, pl.ds(0, side + half + 16))
    share(0, 1, 3)
    row = recv[0, pl.ds(side + half, 16)].astype(F32)
    row = jnp.concatenate([row[0:1], row[8:9, : block - 128]], axis=1)
    ids[0] = row
    columns[0] = jnp.broadcast_to(row, (128, block)).T
    for slot in (5, 7):
        landed(lr_sem, slot, tail)
    share(1, 4, 4)
    shared(0, 1, 3)
    full(0, 2, [])
    full(2, 2, [(0, 2)])
    shared(1, 4, 4)
    arrive(4)
    arrive(5)
    full(4, 2, [(0, 2), (2, 2)])
    arrive(6)
    full(6, 1, [(0, 2), (2, 2), (4, 2)])
    arrive(7)
    def add(acc, pairs):
        for a, na in pairs:
            y, z = product(a, na, 7, 1, True)
            total[pl.ds(a, na)] += y.reshape(na, block, dom)
            acc = acc + z
        return acc

    y = lax.rem(me, 2)
    inside = [jnp.bitwise_xor(lax.rem(me, 4), t) for t in range(4)]

    @pl.when(upper == 0)
    def _():
        acc = add(product(7, 1, 7, 1, False), [(0, 2), (2, 2)])
        offer(0, 0, 4)
        acc = add(acc, [(4, 2)])
        swap(0, 0, 4).wait_recv()
        for a in inside:
            owner(a)
        total[7] = add(acc, [(6, 1)])
        offer(1, 4, 4)
        swap(1, 4, 4).wait_recv()
        for a in range(4, 8):
            owner(a)
        swap(0, 0, 4).wait_send()
        swap(1, 4, 4).wait_send()

    @pl.when(upper == 1)
    def _():
        acc = add(jnp.zeros((block, dom), F32), [(4, 2)])
        offer(0, 4, 2)
        acc = add(acc + product(7, 1, 7, 1, False), [(6, 1), (0, 2)])
        swap(0, 4, 2).wait_recv()
        for a in (4 + y, 5 - y):
            owner(a)
        total[7] = add(acc, [(2, 2)])
        offer(1, 6, 2)
        offer(2, 0, 4)
        swap(1, 6, 2).wait_recv()
        for a in (6, 7):
            owner(a)
        swap(2, 0, 4).wait_recv()
        for a in inside:
            owner(a)
        swap(0, 4, 2).wait_send()
        swap(1, 6, 2).wait_send()
        swap(2, 0, 4).wait_send()

    acc = total[0, mine] + xrecv[0].astype(F32)
    for a in range(1, n):
        remote(rsend.at[a], rrecv.at[a], rs_sem.at[a], rr_sem.at[a], tok=at(1)).wait_recv()
        acc = acc + rrecv[a].astype(F32)
    out[...] = acc
    for a in range(1, n):
        give(a).wait_send()
    for copy in copies:
        copy.wait_send()


def on_device_near_far(acts, grads, losses, sources):
    block, lh, width = acts.shape
    dom = losses.shape[1]
    n = lax.axis_size("tok")
    layers = lh * lax.axis_size("lay")
    scale = 1.0 / math.sqrt(n * block * layers)
    half = block // 2
    dma = pltpu.SemaphoreType.DMA
    pairs = n * block * block * lh
    return pl.pallas_call(
        functools.partial(near_far, scale),
        out_shape=pltpu.VMEM((half, dom), F32),
        in_specs=[pl.BlockSpec(memory_space=pl.ANY)] * 4,
        out_specs=pl.BlockSpec(memory_space=pltpu.VMEM),
        scratch_shapes=[
            pltpu.VMEM((2, block, lh, width), BF16),
            pltpu.VMEM((2, block * lh, width), F32),
            pltpu.VMEM((n, 2 * block + half + 16, width), BF16),
            pltpu.VMEM((n, 2 * block + half + 16, width), BF16),
            pltpu.VMEM((1, block), jnp.int32),
            pltpu.VMEM((n, block, dom), BF16),
            pltpu.VMEM((n, 1, block), F32),
            pltpu.VMEM((n, block, 128), F32),
            pltpu.VMEM((n, block, dom), F32),
            pltpu.VMEM((n, half, dom), BF16),
            pltpu.VMEM((n, half, dom), BF16),
            pltpu.VMEM((n, half, dom), BF16),
            pltpu.VMEM((n, half, dom), BF16),
            dma((n,)), dma((n,)), dma((4,)), dma((n,)), dma((2,)), dma((2,)),
            dma((n,)), dma((n,)), dma((n,)), dma((n,)), dma((4,)),
        ],
        compiler_params=pltpu.CompilerParams(
            collective_id=1, has_side_effects=True, vmem_limit_bytes=56 * 1024 * 1024
        ),
        cost_estimate=pl.CostEstimate(
            flops=2 * pairs * (2 * width + dom), bytes_accessed=4 * block * lh * width, transcendentals=0
        ),
    )(acts, grads, losses, sources.reshape(1, block)) * scale


def solution(mesh):
    placed = (
        P(("grp", "tok"), "lay", None),
        P(("grp", "tok"), "lay", None),
        P(("grp", "tok"), None),
        P(("grp", "tok")),
    )
    def part(acts, grads, losses, sources):
        paired = acts.shape[1] == mesh.shape["tok"] == 8
        return (on_device_near_far if paired else on_device)(acts, grads, losses, sources)

    return jax.shard_map(
        part,
        mesh=mesh,
        in_specs=placed,
        out_specs=P(("grp", "tok", "lay"), None),
        check_vma=False,
    )
```

```python
import functools
import math

import jax
import jax.numpy as jnp
from jax import lax
from jax.experimental import pallas as pl
from jax.experimental.pallas import tpu as pltpu
from jax.sharding import PartitionSpec as P

MESH = pl.DeviceIdType.MESH
F32 = jnp.float32
BF16 = jnp.bfloat16
GROUP = 2


def nt(a, b):
    return lax.dot_general(a, b, (((1,), (1,)), ((), ())), preferred_element_type=F32)


def kernel(
    n, lh, scale,
    acts, grads, losses, sources, out,
    fetched, stage, send, recv, lall, srcs, total, xsend, xrecv, rsend, rrecv,
    send_sem, recv_sem, ls_sem, lr_sem, lf_sem, lx_sem, ly_sem, ss_sem, sr_sem,
    xs_sem, xr_sem, rs_sem, rr_sem, in_sem,
):
    block = acts.shape[0]
    half = block // 2
    sets = n // lh
    me = lax.axis_index("tok")
    h = lax.axis_index("lay")
    q, j = me // lh, lax.rem(me, lh)

    def dest(k):
        return lax.rem(q + sets - k // lh, sets) * lh + jnp.bitwise_xor(j, k % lh)

    mine = pl.ds(pl.multiple_of(h * half, half), half)
    theirs = pl.ds(pl.multiple_of((1 - h) * half, half), half)
    peers = list(range(1, n))
    order = sorted(range(1, lh), key=lambda k: (-(k.bit_length()), k))
    send_order = [kq * lh + kj for kj in order for kq in range(sets)] + [kq * lh for kq in range(1, sets)]

    barrier = pltpu.get_barrier_semaphore()
    for k in peers:
        pl.semaphore_signal(barrier, inc=1, device_id={"tok": dest(k)}, device_id_type=MESH)
    pl.semaphore_signal(barrier, inc=1, device_id={"lay": 1 - h}, device_id_type=MESH)

    local = [
        pltpu.make_async_copy(src, dst, in_sem.at[i])
        for i, (src, dst) in enumerate(
            ((acts, fetched.at[0]), (grads, fetched.at[1]), (losses, lall.at[0]), (sources, srcs.at[0]))
        )
    ]
    for copy in local:
        copy.start()

    def cut(kj):
        layer = jnp.bitwise_xor(j, kj)
        for w in range(2):
            piece = stage[w, pl.ds(layer, block, stride=lh), :].astype(BF16)
            if kj == 0:
                recv[0, w] = piece
            if kj or sets > 1:
                send[kj, w] = piece

    ready = order[: lh // 2]
    for w in range(2):
        local[w].wait()
        stage[w] = fetched[w].astype(F32).reshape(block * lh, acts.shape[2])
    for kj in ready:
        cut(kj)
    for copy in local[2:]:
        copy.wait()
    pl.semaphore_wait(barrier, n)

    def remote(src, dst, s, r, **where):
        return pltpu.make_async_remote_copy(
            src_ref=src, dst_ref=dst, send_sem=s, recv_sem=r, device_id=where, device_id_type=MESH
        )

    copies = []

    def go(copy):
        copy.start()
        copies.append(copy)
        return copy

    first = {}
    for k in send_order:
        if k % 2 == 0:
            first[k] = go(remote(lall.at[0, mine], lall.at[k, mine], ls_sem.at[k], lr_sem.at[k], tok=dest(k)))
    first[1] = go(remote(lall.at[0, mine], lall.at[1, mine], ls_sem.at[1], lr_sem.at[1], tok=dest(1)))
    ids = {}
    for k in send_order:
        ids[k] = go(remote(srcs.at[0], srcs.at[k], ss_sem.at[k], sr_sem.at[k], tok=dest(k)))
    main = {}
    for kj in order + [0]:
        if kj not in ready:
            cut(kj)
        for kq in range(sets):
            k = kq * lh + kj
            if k:
                main[k] = go(remote(send.at[kj], recv.at[k], send_sem.at[k], recv_sem.at[k], tok=dest(k)))

    cross = {}
    for k in range(1, n):
        if k % 2 == 0:
            first[k].wait_recv()
            first[k + 1] = go(
                remote(lall.at[k, mine], lall.at[k + 1, mine], lf_sem.at[k + 1], lr_sem.at[k + 1], tok=dest(1))
            )
            cross[k] = go(remote(lall.at[k, mine], lall.at[k, mine], lx_sem.at[k], ly_sem.at[k], lay=1 - h))
    for k in range(1, n):
        if k % 2 == 1:
            first[k].wait_recv()
            cross[k] = go(remote(lall.at[k, mine], lall.at[k, mine], lx_sem.at[k], ly_sem.at[k], lay=1 - h))

    size = GROUP * block
    flat = (size, acts.shape[2])

    def part(ref_slice):
        return ref_slice.reshape(flat)

    def arrive(g):
        for k in range(g * GROUP, (g + 1) * GROUP):
            if k:
                main[k].wait_recv()
                ids[k].wait_recv()
                cross[k].wait_recv()

    def row_ids(g):
        return jnp.concatenate([srcs[g * GROUP + i] for i in range(GROUP)], axis=1)

    rows = {}
    cols = {}

    def one(a, b, both=False):
        sa, sb = pl.ds(a * GROUP, GROUP), pl.ds(b * GROUP, GROUP)
        x = nt(part(recv[sa, 0]), part(recv[sb, 0])) * nt(part(recv[sa, 1]), part(recv[sb, 1]))
        col = cols[a]
        reps = size // col.shape[1]
        keep = jnp.concatenate([col] * reps, axis=1) != rows[b]
        x = jnp.where(keep, x, 0.0).astype(BF16)
        y = jnp.dot(x, lall[sb].reshape(size, losses.shape[1]), preferred_element_type=F32)
        if not both:
            return y
        z = lax.dot_general(x, lall[sa].reshape(size, losses.shape[1]), (((0,), (0,)), ((), ())), preferred_element_type=F32)
        return y, z

    dom = losses.shape[1]

    def add(a, b):
        total[pl.ds(a * GROUP, GROUP)] += one(a, b).reshape(GROUP, block, dom)

    def full(g, after=None):
        acc = one(g, g)
        for a in sorted(range(g), key=lambda a: (-(a.bit_length()), a)):
            y, z = one(a, g, True)
            total[pl.ds(a * GROUP, GROUP)] += y.reshape(GROUP, block, dom)
            acc = acc + z
            if after and a == g - 1:
                after(a)
        total[pl.ds(g * GROUP, GROUP)] = acc.reshape(GROUP, block, dom)

    swaps = {}
    back = {}

    def swap(a):
        at = pl.ds(a * GROUP, GROUP)
        xsend[at] = total[at, theirs].astype(BF16)
        swaps[a] = go(remote(xsend.at[at], xrecv.at[at], xs_sem.at[a], xr_sem.at[a], lay=1 - h))

    def owners(a):
        swaps[a].wait_recv()
        for k in range(a * GROUP, (a + 1) * GROUP):
            if k:
                rsend[k] = (total[k, mine] + xrecv[k].astype(F32)).astype(BF16)
                back[k] = go(remote(rsend.at[k], rrecv.at[k], rs_sem.at[k], rr_sem.at[k], tok=dest(k)))

    groups = lh // GROUP
    last = groups - 1
    for g in range(groups):
        arrive(g)
        rows[g] = row_ids(g)
        cols[g] = jnp.broadcast_to(rows[g], (128, size)).T
        if g == last and sets == 1:
            break
        full(g)
    if sets > 1:
        for g in range(groups, n // GROUP):
            arrive(g)

        @pl.loop(groups, n // GROUP)
        def _(g):
            there = jnp.concatenate([srcs[g * GROUP + i] for i in range(GROUP)], axis=1)
            sb = pl.ds(g * GROUP, GROUP)
            for a in range(groups):
                sa = pl.ds(a * GROUP, GROUP)
                x = nt(part(recv[sa, 0]), part(recv[sb, 0])) * nt(part(recv[sa, 1]), part(recv[sb, 1]))
                col = jnp.broadcast_to(row_ids(a), (128, size)).T
                keep = jnp.concatenate([col] * (size // 128), axis=1) != there
                x = jnp.where(keep, x, 0.0).astype(BF16)
                y = jnp.dot(x, lall[sb].reshape(size, dom), preferred_element_type=F32)
                total[sa] += y.reshape(GROUP, block, dom)

    turn = sorted(range(groups), key=lambda a: (-(a.bit_length()), a))
    for i, a in enumerate(turn):
        if i == 0 and sets == 1:
            full(last, swap)
            for a in turn[1:]:
                swap(a)
        elif sets > 1:
            swap(a)
    for a in turn:
        owners(a)
    acc = total[0, mine] + xrecv[0].astype(F32)
    for k in order[::-1]:
        back[k].wait_recv()
        acc = acc + rrecv[k].astype(F32)
    out[...] = acc * scale
    for copy in copies:
        copy.wait_send()


def on_device(acts, grads, losses, sources):
    block, lh, width = acts.shape
    dom = losses.shape[1]
    n = lax.axis_size("tok")
    layers = lh * lax.axis_size("lay")
    scale = 1.0 / math.sqrt(n * block * layers)
    half = block // 2
    dma = pltpu.SemaphoreType.DMA
    vmem = pl.BlockSpec(memory_space=pltpu.VMEM)
    pairs = n * block * block * lh
    return pl.pallas_call(
        functools.partial(kernel, n, lh, scale),
        out_shape=jax.ShapeDtypeStruct((half, dom), F32),
        in_specs=[pl.BlockSpec(memory_space=pl.ANY)] * 4,
        out_specs=vmem,
        scratch_shapes=[
            pltpu.VMEM((2, block, lh, width), BF16),
            pltpu.VMEM((2, block * lh, width), F32),
            pltpu.VMEM((lh, 2, block, width), BF16),
            pltpu.VMEM((n, 2, block, width), BF16),
            pltpu.VMEM((n, block, dom), BF16),
            pltpu.VMEM((n, 1, block), jnp.int32),
            pltpu.VMEM((lh, block, dom), F32),
            pltpu.VMEM((lh, half, dom), BF16),
            pltpu.VMEM((lh, half, dom), BF16),
            pltpu.VMEM((lh, half, dom), BF16),
            pltpu.VMEM((lh, half, dom), BF16),
            dma((n,)), dma((n,)), dma((n,)), dma((n,)), dma((n,)), dma((n,)), dma((n,)), dma((n,)), dma((n,)),
            dma((lh,)), dma((lh,)), dma((lh,)), dma((lh,)), dma((4,)),
        ],
        compiler_params=pltpu.CompilerParams(
            collective_id=0, has_side_effects=True, vmem_limit_bytes=56 * 1024 * 1024
        ),
        cost_estimate=pl.CostEstimate(
            flops=2 * pairs * (2 * width + dom), bytes_accessed=4 * block * lh * width, transcendentals=0
        ),
    )(acts, grads, losses, sources.reshape(1, block))


def near_far(
    scale,
    acts, grads, losses, sources, out,
    fetched, stage, send, recv, own, lall, ids, columns, total, xsend, xrecv, rsend, rrecv,
    send_sem, recv_sem, ls_sem, lr_sem, lx_sem, ly_sem, xs_sem, xr_sem, rs_sem, rr_sem, in_sem,
):
    block, lh, width = acts.shape
    dom = losses.shape[1]
    half = block // 2
    n = 8
    me = lax.axis_index("tok")
    h = lax.axis_index("lay")
    upper = me // 4
    odd = lax.rem(me // 2, 2)
    inner = jnp.bitwise_xor(odd, upper)
    outer = 1 - inner
    mine = pl.ds(pl.multiple_of(h * half, half), half)
    theirs = pl.ds(pl.multiple_of((1 - h) * half, half), half)

    def at(k):
        return jnp.bitwise_xor(me, k)

    barrier = pltpu.get_barrier_semaphore()
    for k in range(n - 1, 0, -1):
        pl.semaphore_signal(barrier, inc=1, device_id={"tok": at(k)}, device_id_type=MESH)
    pl.semaphore_signal(barrier, inc=1, device_id={"lay": 1 - h}, device_id_type=MESH)

    local = [
        pltpu.make_async_copy(src, dst, in_sem.at[i])
        for i, (src, dst) in enumerate(
            ((losses, lall.at[0]), (sources, own), (acts, fetched.at[0]), (grads, fetched.at[1]))
        )
    ]
    for copy in local:
        copy.start()

    def remote(src, dst, s, r, **where):
        return pltpu.make_async_remote_copy(
            src_ref=src, dst_ref=dst, send_sem=s, recv_sem=r, device_id=where, device_id_type=MESH
        )

    copies = []

    def go(copy):
        copy.start()
        copies.append(copy)
        return copy

    side = 2 * block
    tail = pl.ds(side, half + 16)

    def cut(i, layer):
        for w in range(2):
            send[i, pl.ds(w * block, block)] = stage[w, pl.ds(layer, block, stride=lh), :].astype(BF16)

    for copy in local[:2]:
        copy.wait()
    row = jnp.concatenate([own[...], jnp.zeros((1, 256 - block), jnp.int32)], axis=1).astype(F32)
    row = jnp.concatenate([jnp.broadcast_to(row[:, :128], (8, 128)), jnp.broadcast_to(row[:, 128:], (8, 128))])
    note = jnp.concatenate([lall[0, mine], row.astype(BF16)])
    for k in range(4):
        send[k, tail] = note

    far = [4 + t for t in range(4)]
    for w in range(2):
        local[2 + w].wait()
        stage[w] = fetched[w].astype(F32).reshape(block * lh, width)
    for t in range(4):
        cut(4 + t, at(far[t]))
    pl.semaphore_wait(barrier, n)

    across = 4 + 2 * inner
    body = pl.ds(0, side)

    def mail(i, k, slot, where):
        return remote(send.at[i, where], recv.at[slot, where], send_sem.at[i], recv_sem.at[slot], tok=at(k))

    def note_to(i, k):
        return remote(send.at[0, tail], recv.at[across, tail], ls_sem.at[i], lr_sem.at[across], tok=at(k))

    for i, k in enumerate((4, 6)):
        go(note_to(i, k))
    for t in range(4):
        go(mail(4 + t, far[t], across + t % 2, body))
    for k in range(1, 4):
        cut(k, at(k))
        go(mail(k, k, k, pl.ds(0, side + half + 16)))
    for w in range(2):
        recv[0, pl.ds(w * block, block)] = stage[w, pl.ds(me, block, stride=lh), :].astype(BF16)
    recv[0, tail] = note

    def landed(sem, slot, where):
        remote(recv.at[slot, where], recv.at[slot, where], ls_sem.at[0], sem.at[slot], tok=at(1)).wait_recv()

    for i, slot in enumerate((4, 6)):
        landed(lr_sem, slot, tail)
        go(remote(recv.at[slot, tail], recv.at[slot + 1, tail], ls_sem.at[2 + i], lr_sem.at[slot + 1], tok=at(1)))

    loss_rows = pl.ds(side, half)

    def share(i, first, count):
        slots = pl.ds(first, count)
        go(remote(recv.at[slots, loss_rows], lall.at[slots, mine], lx_sem.at[i], ly_sem.at[i], lay=1 - h))
        lall[slots, mine] = recv[slots, loss_rows]
        for slot in range(first, first + count):
            row = recv[slot, pl.ds(side + half, 16)].astype(F32)
            row = jnp.concatenate([row[0:1], row[8:9, : block - 128]], axis=1)
            ids[slot] = row
            columns[slot] = jnp.broadcast_to(row, (128, block)).T

    def shared(i, first, count):
        slots = pl.ds(first, count)
        remote(recv.at[slots, loss_rows], lall.at[slots, theirs], lx_sem.at[i], ly_sem.at[i], lay=1 - h).wait_recv()

    def arrive(slot):
        if slot > 3:
            landed(recv_sem, slot, body)

    def product(a, na, b, nb, both):
        sa, sb = pl.ds(a, na), pl.ds(b, nb)
        ra, rb = na * block, nb * block
        x = nt(recv[sa, :block].reshape(ra, width), recv[sb, :block].reshape(rb, width))
        x = x * nt(recv[sa, block:side].reshape(ra, width), recv[sb, block:side].reshape(rb, width))
        col = columns[sa].reshape(ra, 128)
        col = jnp.concatenate([col] * -(-rb // 128), axis=1)[:, :rb]
        row = ids[b] if nb == 1 else jnp.concatenate([ids[b + i] for i in range(nb)], axis=1)
        x = jnp.where(col != row, x, 0.0).astype(BF16)
        y = jnp.dot(x, lall[sb].reshape(rb, dom), preferred_element_type=F32)
        if not both:
            return y
        z = lax.dot_general(x, lall[sa].reshape(ra, dom), (((0,), (0,)), ((), ())), preferred_element_type=F32)
        return y, z

    def full(b, nb, before):
        acc = product(b, nb, b, nb, False)
        for a, na in before:
            y, z = product(a, na, b, nb, True)
            total[pl.ds(a, na)] += y.reshape(na, block, dom)
            acc = acc + z
        total[pl.ds(b, nb)] = acc.reshape(nb, block, dom)

    def swap(i, first, count):
        slots = pl.ds(first, count)
        return remote(xsend.at[slots], xrecv.at[slots], xs_sem.at[i], xr_sem.at[i], lay=1 - h)

    def offer(i, first, count):
        slots = pl.ds(first, count)
        xsend[slots] = total[slots, theirs].astype(BF16)
        swap(i, first, count).start()

    def owner(a):
        @pl.when(a != 0)
        def _():
            rsend[a] = (total[a, mine] + xrecv[a].astype(F32)).astype(BF16)
            give(a).start()

    def give(a):
        far = a // 4
        p = lax.rem(a, 2)
        k = jnp.where(far == 1, 4 + p + 2 * jnp.bitwise_xor(lax.rem(a // 2, 2), outer), a)
        to = jnp.where(far == 1, across + p, a)
        return remote(rsend.at[a], rrecv.at[to], rs_sem.at[a], rr_sem.at[to], tok=at(k))

    for slot in (1, 2, 3):
        landed(recv_sem, slot, pl.ds(0, side + half + 16))
    share(0, 1, 3)
    row = recv[0, pl.ds(side + half, 16)].astype(F32)
    row = jnp.concatenate([row[0:1], row[8:9, : block - 128]], axis=1)
    ids[0] = row
    columns[0] = jnp.broadcast_to(row, (128, block)).T
    for slot in (5, 7):
        landed(lr_sem, slot, tail)
    share(1, 4, 4)
    shared(0, 1, 3)
    full(0, 2, [])
    full(2, 2, [(0, 2)])
    shared(1, 4, 4)
    arrive(4)
    arrive(5)
    full(4, 2, [(0, 2), (2, 2)])
    arrive(6)
    full(6, 1, [(0, 2), (2, 2), (4, 2)])
    arrive(7)
    def add(acc, pairs):
        for a, na in pairs:
            y, z = product(a, na, 7, 1, True)
            total[pl.ds(a, na)] += y.reshape(na, block, dom)
            acc = acc + z
        return acc

    y = lax.rem(me, 2)
    inside = [jnp.bitwise_xor(lax.rem(me, 4), t) for t in range(4)]

    @pl.when(upper == 0)
    def _():
        first = 2 * odd
        acc = add(jnp.zeros((block, dom), F32), [(first, 2)])
        offer(0, first, 2)
        acc = add(acc + product(7, 1, 7, 1, False), [(2 - first, 2), (4, 2)])
        swap(0, first, 2).wait_recv()
        for a in inside[:2]:
            owner(a)
        offer(1, 2 - first, 2)
        total[7] = add(acc, [(6, 1)])
        offer(2, 4, 4)
        swap(1, 2 - first, 2).wait_recv()
        for a in inside[2:]:
            owner(a)
        swap(2, 4, 4).wait_recv()
        for a in range(4, 8):
            owner(a)
        swap(0, first, 2).wait_send()
        swap(1, 2 - first, 2).wait_send()
        swap(2, 4, 4).wait_send()

    @pl.when(upper == 1)
    def _():
        acc = add(jnp.zeros((block, dom), F32), [(4, 2)])
        offer(0, 4, 2)
        acc = add(acc + product(7, 1, 7, 1, False), [(6, 1), (0, 2)])
        swap(0, 4, 2).wait_recv()
        owner(4 + y)
        total[7] = add(acc, [(2, 2)])
        offer(1, 6, 2)
        offer(2, 0, 4)
        owner(5 - y)
        swap(1, 6, 2).wait_recv()
        for a in (6, 7):
            owner(a)
        swap(2, 0, 4).wait_recv()
        for a in inside:
            owner(a)
        swap(0, 4, 2).wait_send()
        swap(1, 6, 2).wait_send()
        swap(2, 0, 4).wait_send()

    acc = total[0, mine] + xrecv[0].astype(F32)
    for a in range(1, n):
        remote(rsend.at[a], rrecv.at[a], rs_sem.at[a], rr_sem.at[a], tok=at(1)).wait_recv()
        acc = acc + rrecv[a].astype(F32)
    out[...] = acc
    for a in range(1, n):
        give(a).wait_send()
    for copy in copies:
        copy.wait_send()


def on_device_near_far(acts, grads, losses, sources):
    block, lh, width = acts.shape
    dom = losses.shape[1]
    n = lax.axis_size("tok")
    layers = lh * lax.axis_size("lay")
    scale = 1.0 / math.sqrt(n * block * layers)
    half = block // 2
    dma = pltpu.SemaphoreType.DMA
    pairs = n * block * block * lh
    return pl.pallas_call(
        functools.partial(near_far, scale),
        out_shape=pltpu.VMEM((half, dom), F32),
        in_specs=[pl.BlockSpec(memory_space=pl.ANY)] * 4,
        out_specs=pl.BlockSpec(memory_space=pltpu.VMEM),
        scratch_shapes=[
            pltpu.VMEM((2, block, lh, width), BF16),
            pltpu.VMEM((2, block * lh, width), F32),
            pltpu.VMEM((n, 2 * block + half + 16, width), BF16),
            pltpu.VMEM((n, 2 * block + half + 16, width), BF16),
            pltpu.VMEM((1, block), jnp.int32),
            pltpu.VMEM((n, block, dom), BF16),
            pltpu.VMEM((n, 1, block), F32),
            pltpu.VMEM((n, block, 128), F32),
            pltpu.VMEM((n, block, dom), F32),
            pltpu.VMEM((n, half, dom), BF16),
            pltpu.VMEM((n, half, dom), BF16),
            pltpu.VMEM((n, half, dom), BF16),
            pltpu.VMEM((n, half, dom), BF16),
            dma((n,)), dma((n,)), dma((4,)), dma((n,)), dma((2,)), dma((2,)),
            dma((n,)), dma((n,)), dma((n,)), dma((n,)), dma((4,)),
        ],
        compiler_params=pltpu.CompilerParams(
            collective_id=1, has_side_effects=True, vmem_limit_bytes=56 * 1024 * 1024
        ),
        cost_estimate=pl.CostEstimate(
            flops=2 * pairs * (2 * width + dom), bytes_accessed=4 * block * lh * width, transcendentals=0
        ),
    )(acts, grads, losses, sources.reshape(1, block)) * scale


def solution(mesh):
    placed = (
        P(("grp", "tok"), "lay", None),
        P(("grp", "tok"), "lay", None),
        P(("grp", "tok"), None),
        P(("grp", "tok")),
    )
    def part(acts, grads, losses, sources):
        paired = acts.shape[1] == mesh.shape["tok"] == 8
        return (on_device_near_far if paired else on_device)(acts, grads, losses, sources)

    return jax.shard_map(
        part,
        mesh=mesh,
        in_specs=placed,
        out_specs=P(("grp", "tok", "lay"), None),
        check_vma=False,
    )
```

```python
import functools
import math

import jax
import jax.numpy as jnp
from jax import lax
from jax.experimental import pallas as pl
from jax.experimental.pallas import tpu as pltpu
from jax.sharding import PartitionSpec as P

MESH = pl.DeviceIdType.MESH
F32 = jnp.float32
BF16 = jnp.bfloat16
GROUP = 2


def nt(a, b):
    return lax.dot_general(a, b, (((1,), (1,)), ((), ())), preferred_element_type=F32)


def kernel(
    n, lh, scale,
    acts, grads, losses, sources, out,
    fetched, stage, send, recv, lall, srcs, total, xsend, xrecv, rsend, rrecv,
    send_sem, recv_sem, ls_sem, lr_sem, lf_sem, lx_sem, ly_sem, ss_sem, sr_sem,
    xs_sem, xr_sem, rs_sem, rr_sem, in_sem,
):
    block = acts.shape[0]
    half = block // 2
    sets = n // lh
    me = lax.axis_index("tok")
    h = lax.axis_index("lay")
    q, j = me // lh, lax.rem(me, lh)

    def dest(k):
        return lax.rem(q + sets - k // lh, sets) * lh + jnp.bitwise_xor(j, k % lh)

    mine = pl.ds(pl.multiple_of(h * half, half), half)
    theirs = pl.ds(pl.multiple_of((1 - h) * half, half), half)
    peers = list(range(1, n))
    order = sorted(range(1, lh), key=lambda k: (-(k.bit_length()), k))
    send_order = [kq * lh + kj for kj in order for kq in range(sets)] + [kq * lh for kq in range(1, sets)]

    barrier = pltpu.get_barrier_semaphore()
    for k in peers:
        pl.semaphore_signal(barrier, inc=1, device_id={"tok": dest(k)}, device_id_type=MESH)
    pl.semaphore_signal(barrier, inc=1, device_id={"lay": 1 - h}, device_id_type=MESH)

    local = [
        pltpu.make_async_copy(src, dst, in_sem.at[i])
        for i, (src, dst) in enumerate(
            ((acts, fetched.at[0]), (grads, fetched.at[1]), (losses, lall.at[0]), (sources, srcs.at[0]))
        )
    ]
    for copy in local:
        copy.start()

    def cut(kj):
        layer = jnp.bitwise_xor(j, kj)
        for w in range(2):
            piece = stage[w, pl.ds(layer, block, stride=lh), :].astype(BF16)
            if kj == 0:
                recv[0, w] = piece
            if kj or sets > 1:
                send[kj, w] = piece

    ready = order[: lh // 2]
    for w in range(2):
        local[w].wait()
        stage[w] = fetched[w].astype(F32).reshape(block * lh, acts.shape[2])
    for kj in ready:
        cut(kj)
    for copy in local[2:]:
        copy.wait()
    pl.semaphore_wait(barrier, n)

    def remote(src, dst, s, r, **where):
        return pltpu.make_async_remote_copy(
            src_ref=src, dst_ref=dst, send_sem=s, recv_sem=r, device_id=where, device_id_type=MESH
        )

    copies = []

    def go(copy):
        copy.start()
        copies.append(copy)
        return copy

    first = {}
    for k in send_order:
        if k % 2 == 0:
            first[k] = go(remote(lall.at[0, mine], lall.at[k, mine], ls_sem.at[k], lr_sem.at[k], tok=dest(k)))
    first[1] = go(remote(lall.at[0, mine], lall.at[1, mine], ls_sem.at[1], lr_sem.at[1], tok=dest(1)))
    ids = {}
    for k in send_order:
        ids[k] = go(remote(srcs.at[0], srcs.at[k], ss_sem.at[k], sr_sem.at[k], tok=dest(k)))
    main = {}
    for kj in order + [0]:
        if kj not in ready:
            cut(kj)
        for kq in range(sets):
            k = kq * lh + kj
            if k:
                main[k] = go(remote(send.at[kj], recv.at[k], send_sem.at[k], recv_sem.at[k], tok=dest(k)))

    cross = {}
    for k in range(1, n):
        if k % 2 == 0:
            first[k].wait_recv()
            first[k + 1] = go(
                remote(lall.at[k, mine], lall.at[k + 1, mine], lf_sem.at[k + 1], lr_sem.at[k + 1], tok=dest(1))
            )
            cross[k] = go(remote(lall.at[k, mine], lall.at[k, mine], lx_sem.at[k], ly_sem.at[k], lay=1 - h))
    for k in range(1, n):
        if k % 2 == 1:
            first[k].wait_recv()
            cross[k] = go(remote(lall.at[k, mine], lall.at[k, mine], lx_sem.at[k], ly_sem.at[k], lay=1 - h))

    size = GROUP * block
    flat = (size, acts.shape[2])

    def part(ref_slice):
        return ref_slice.reshape(flat)

    def arrive(g):
        for k in range(g * GROUP, (g + 1) * GROUP):
            if k:
                main[k].wait_recv()
                ids[k].wait_recv()
                cross[k].wait_recv()

    def row_ids(g):
        return jnp.concatenate([srcs[g * GROUP + i] for i in range(GROUP)], axis=1)

    rows = {}
    cols = {}

    def one(a, b, both=False):
        sa, sb = pl.ds(a * GROUP, GROUP), pl.ds(b * GROUP, GROUP)
        x = nt(part(recv[sa, 0]), part(recv[sb, 0])) * nt(part(recv[sa, 1]), part(recv[sb, 1]))
        col = cols[a]
        reps = size // col.shape[1]
        keep = jnp.concatenate([col] * reps, axis=1) != rows[b]
        x = jnp.where(keep, x, 0.0).astype(BF16)
        y = jnp.dot(x, lall[sb].reshape(size, losses.shape[1]), preferred_element_type=F32)
        if not both:
            return y
        z = lax.dot_general(x, lall[sa].reshape(size, losses.shape[1]), (((0,), (0,)), ((), ())), preferred_element_type=F32)
        return y, z

    dom = losses.shape[1]

    def add(a, b):
        total[pl.ds(a * GROUP, GROUP)] += one(a, b).reshape(GROUP, block, dom)

    def full(g, after=None):
        acc = one(g, g)
        for a in sorted(range(g), key=lambda a: (-(a.bit_length()), a)):
            y, z = one(a, g, True)
            total[pl.ds(a * GROUP, GROUP)] += y.reshape(GROUP, block, dom)
            acc = acc + z
            if after and a == g - 1:
                after(a)
        total[pl.ds(g * GROUP, GROUP)] = acc.reshape(GROUP, block, dom)

    swaps = {}
    back = {}

    def swap(a):
        at = pl.ds(a * GROUP, GROUP)
        xsend[at] = total[at, theirs].astype(BF16)
        swaps[a] = go(remote(xsend.at[at], xrecv.at[at], xs_sem.at[a], xr_sem.at[a], lay=1 - h))

    def owners(a):
        swaps[a].wait_recv()
        for k in range(a * GROUP, (a + 1) * GROUP):
            if k:
                rsend[k] = (total[k, mine] + xrecv[k].astype(F32)).astype(BF16)
                back[k] = go(remote(rsend.at[k], rrecv.at[k], rs_sem.at[k], rr_sem.at[k], tok=dest(k)))

    groups = lh // GROUP
    last = groups - 1
    for g in range(groups):
        arrive(g)
        rows[g] = row_ids(g)
        cols[g] = jnp.broadcast_to(rows[g], (128, size)).T
        if g == last and sets == 1:
            break
        full(g)
    if sets > 1:
        for g in range(groups, n // GROUP):
            arrive(g)

        @pl.loop(groups, n // GROUP)
        def _(g):
            there = jnp.concatenate([srcs[g * GROUP + i] for i in range(GROUP)], axis=1)
            sb = pl.ds(g * GROUP, GROUP)
            for a in range(groups):
                sa = pl.ds(a * GROUP, GROUP)
                x = nt(part(recv[sa, 0]), part(recv[sb, 0])) * nt(part(recv[sa, 1]), part(recv[sb, 1]))
                col = jnp.broadcast_to(row_ids(a), (128, size)).T
                keep = jnp.concatenate([col] * (size // 128), axis=1) != there
                x = jnp.where(keep, x, 0.0).astype(BF16)
                y = jnp.dot(x, lall[sb].reshape(size, dom), preferred_element_type=F32)
                total[sa] += y.reshape(GROUP, block, dom)

    turn = sorted(range(groups), key=lambda a: (-(a.bit_length()), a))
    for i, a in enumerate(turn):
        if i == 0 and sets == 1:
            full(last, swap)
            for a in turn[1:]:
                swap(a)
        elif sets > 1:
            swap(a)
    for a in turn:
        owners(a)
    acc = total[0, mine] + xrecv[0].astype(F32)
    for k in order[::-1]:
        back[k].wait_recv()
        acc = acc + rrecv[k].astype(F32)
    out[...] = acc * scale
    for copy in copies:
        copy.wait_send()


def on_device(acts, grads, losses, sources):
    block, lh, width = acts.shape
    dom = losses.shape[1]
    n = lax.axis_size("tok")
    layers = lh * lax.axis_size("lay")
    scale = 1.0 / math.sqrt(n * block * layers)
    half = block // 2
    dma = pltpu.SemaphoreType.DMA
    vmem = pl.BlockSpec(memory_space=pltpu.VMEM)
    pairs = n * block * block * lh
    return pl.pallas_call(
        functools.partial(kernel, n, lh, scale),
        out_shape=jax.ShapeDtypeStruct((half, dom), F32),
        in_specs=[pl.BlockSpec(memory_space=pl.ANY)] * 4,
        out_specs=vmem,
        scratch_shapes=[
            pltpu.VMEM((2, block, lh, width), BF16),
            pltpu.VMEM((2, block * lh, width), F32),
            pltpu.VMEM((lh, 2, block, width), BF16),
            pltpu.VMEM((n, 2, block, width), BF16),
            pltpu.VMEM((n, block, dom), BF16),
            pltpu.VMEM((n, 1, block), jnp.int32),
            pltpu.VMEM((lh, block, dom), F32),
            pltpu.VMEM((lh, half, dom), BF16),
            pltpu.VMEM((lh, half, dom), BF16),
            pltpu.VMEM((lh, half, dom), BF16),
            pltpu.VMEM((lh, half, dom), BF16),
            dma((n,)), dma((n,)), dma((n,)), dma((n,)), dma((n,)), dma((n,)), dma((n,)), dma((n,)), dma((n,)),
            dma((lh,)), dma((lh,)), dma((lh,)), dma((lh,)), dma((4,)),
        ],
        compiler_params=pltpu.CompilerParams(
            collective_id=0, has_side_effects=True, vmem_limit_bytes=56 * 1024 * 1024
        ),
        cost_estimate=pl.CostEstimate(
            flops=2 * pairs * (2 * width + dom), bytes_accessed=4 * block * lh * width, transcendentals=0
        ),
    )(acts, grads, losses, sources.reshape(1, block))


def near_far(
    scale,
    acts, grads, losses, sources, out,
    fetched, stage, send, recv, own, lall, ids, columns, total, xsend, xrecv, rsend, rrecv,
    send_sem, recv_sem, ls_sem, lr_sem, lx_sem, ly_sem, xs_sem, xr_sem, rs_sem, rr_sem, in_sem,
):
    block, lh, width = acts.shape
    dom = losses.shape[1]
    half = block // 2
    n = 8
    me = lax.axis_index("tok")
    h = lax.axis_index("lay")
    upper = me // 4
    odd = lax.rem(me // 2, 2)
    inner = jnp.bitwise_xor(odd, upper)
    outer = 1 - inner
    mine = pl.ds(pl.multiple_of(h * half, half), half)
    theirs = pl.ds(pl.multiple_of((1 - h) * half, half), half)

    def at(k):
        return jnp.bitwise_xor(me, k)

    barrier = pltpu.get_barrier_semaphore()
    for k in range(n - 1, 0, -1):
        pl.semaphore_signal(barrier, inc=1, device_id={"tok": at(k)}, device_id_type=MESH)
    pl.semaphore_signal(barrier, inc=1, device_id={"lay": 1 - h}, device_id_type=MESH)

    local = [
        pltpu.make_async_copy(src, dst, in_sem.at[i])
        for i, (src, dst) in enumerate(
            ((losses, lall.at[0]), (sources, own), (acts, fetched.at[0]), (grads, fetched.at[1]))
        )
    ]
    for copy in local:
        copy.start()

    def remote(src, dst, s, r, **where):
        return pltpu.make_async_remote_copy(
            src_ref=src, dst_ref=dst, send_sem=s, recv_sem=r, device_id=where, device_id_type=MESH
        )

    copies = []

    def go(copy):
        copy.start()
        copies.append(copy)
        return copy

    side = 2 * block
    tail = pl.ds(side, half + 16)

    def cut(i, layer):
        for w in range(2):
            send[i, pl.ds(w * block, block)] = stage[w, pl.ds(layer, block, stride=lh), :].astype(BF16)

    for copy in local[:2]:
        copy.wait()
    row = jnp.concatenate([own[...], jnp.zeros((1, 256 - block), jnp.int32)], axis=1).astype(F32)
    row = jnp.concatenate([jnp.broadcast_to(row[:, :128], (8, 128)), jnp.broadcast_to(row[:, 128:], (8, 128))])
    note = jnp.concatenate([lall[0, mine], row.astype(BF16)])
    for k in range(4):
        send[k, tail] = note

    far = [4 + t for t in range(4)]
    for w in range(2):
        local[2 + w].wait()
        stage[w] = fetched[w].astype(F32).reshape(block * lh, width)
    for t in range(4):
        cut(4 + t, at(far[t]))
    pl.semaphore_wait(barrier, n)

    across = 4 + 2 * inner
    body = pl.ds(0, side)

    def mail(i, k, slot, where):
        return remote(send.at[i, where], recv.at[slot, where], send_sem.at[i], recv_sem.at[slot], tok=at(k))

    def note_to(i, k):
        return remote(send.at[0, tail], recv.at[across, tail], ls_sem.at[i], lr_sem.at[across], tok=at(k))

    for i, k in enumerate((4, 6)):
        go(note_to(i, k))
    for t in range(4):
        go(mail(4 + t, far[t], across + t % 2, body))
    for k in range(1, 4):
        cut(k, at(k))
        go(mail(k, k, k, pl.ds(0, side + half + 16)))
    for w in range(2):
        recv[0, pl.ds(w * block, block)] = stage[w, pl.ds(me, block, stride=lh), :].astype(BF16)
    recv[0, tail] = note

    def landed(sem, slot, where):
        remote(recv.at[slot, where], recv.at[slot, where], ls_sem.at[0], sem.at[slot], tok=at(1)).wait_recv()

    for i, slot in enumerate((4, 6)):
        landed(lr_sem, slot, tail)
        go(remote(recv.at[slot, tail], recv.at[slot + 1, tail], ls_sem.at[2 + i], lr_sem.at[slot + 1], tok=at(1)))

    loss_rows = pl.ds(side, half)

    def share(i, first, count):
        slots = pl.ds(first, count)
        go(remote(recv.at[slots, loss_rows], lall.at[slots, mine], lx_sem.at[i], ly_sem.at[i], lay=1 - h))
        lall[slots, mine] = recv[slots, loss_rows]
        for slot in range(first, first + count):
            row = recv[slot, pl.ds(side + half, 16)].astype(F32)
            row = jnp.concatenate([row[0:1], row[8:9, : block - 128]], axis=1)
            ids[slot] = row
            columns[slot] = jnp.broadcast_to(row, (128, block)).T

    def shared(i, first, count):
        slots = pl.ds(first, count)
        remote(recv.at[slots, loss_rows], lall.at[slots, theirs], lx_sem.at[i], ly_sem.at[i], lay=1 - h).wait_recv()

    def arrive(slot):
        if slot > 3:
            landed(recv_sem, slot, body)

    def product(a, na, b, nb, both):
        sa, sb = pl.ds(a, na), pl.ds(b, nb)
        ra, rb = na * block, nb * block
        x = nt(recv[sa, :block].reshape(ra, width), recv[sb, :block].reshape(rb, width))
        x = x * nt(recv[sa, block:side].reshape(ra, width), recv[sb, block:side].reshape(rb, width))
        col = columns[sa].reshape(ra, 128)
        col = jnp.concatenate([col] * -(-rb // 128), axis=1)[:, :rb]
        row = ids[b] if nb == 1 else jnp.concatenate([ids[b + i] for i in range(nb)], axis=1)
        x = jnp.where(col != row, x, 0.0).astype(BF16)
        y = jnp.dot(x, lall[sb].reshape(rb, dom), preferred_element_type=F32)
        if not both:
            return y
        z = lax.dot_general(x, lall[sa].reshape(ra, dom), (((0,), (0,)), ((), ())), preferred_element_type=F32)
        return y, z

    def full(b, nb, before):
        acc = product(b, nb, b, nb, False)
        for a, na in before:
            y, z = product(a, na, b, nb, True)
            total[pl.ds(a, na)] += y.reshape(na, block, dom)
            acc = acc + z
        total[pl.ds(b, nb)] = acc.reshape(nb, block, dom)

    def swap(i, first, count):
        slots = pl.ds(first, count)
        return remote(xsend.at[slots], xrecv.at[slots], xs_sem.at[i], xr_sem.at[i], lay=1 - h)

    def offer(i, first, count):
        slots = pl.ds(first, count)
        xsend[slots] = total[slots, theirs].astype(BF16)
        swap(i, first, count).start()

    def owner(a):
        @pl.when(a != 0)
        def _():
            rsend[a] = (total[a, mine] + xrecv[a].astype(F32)).astype(BF16)
            give(a).start()

    def give(a):
        far = a // 4
        p = lax.rem(a, 2)
        k = jnp.where(far == 1, 4 + p + 2 * jnp.bitwise_xor(lax.rem(a // 2, 2), outer), a)
        to = jnp.where(far == 1, across + p, a)
        return remote(rsend.at[a], rrecv.at[to], rs_sem.at[a], rr_sem.at[to], tok=at(k))

    for slot in (1, 2, 3):
        landed(recv_sem, slot, pl.ds(0, side + half + 16))
    share(0, 1, 3)
    row = recv[0, pl.ds(side + half, 16)].astype(F32)
    row = jnp.concatenate([row[0:1], row[8:9, : block - 128]], axis=1)
    ids[0] = row
    columns[0] = jnp.broadcast_to(row, (128, block)).T
    landed(lr_sem, 5, tail)
    share(1, 4, 2)
    shared(0, 1, 3)
    full(0, 2, [])
    full(2, 2, [(0, 2)])
    shared(1, 4, 2)
    arrive(4)
    arrive(5)
    full(4, 2, [(0, 2), (2, 2)])
    landed(lr_sem, 7, tail)
    share(2, 6, 2)
    shared(2, 6, 2)
    arrive(6)
    full(6, 1, [(0, 2), (2, 2), (4, 2)])
    arrive(7)
    def add(acc, pairs):
        for a, na in pairs:
            y, z = product(a, na, 7, 1, True)
            total[pl.ds(a, na)] += y.reshape(na, block, dom)
            acc = acc + z
        return acc

    y = lax.rem(me, 2)
    inside = [jnp.bitwise_xor(lax.rem(me, 4), t) for t in range(4)]

    @pl.when(upper == 0)
    def _():
        first = 2 * odd
        acc = add(jnp.zeros((block, dom), F32), [(first, 2)])
        offer(0, first, 2)
        acc = add(acc + product(7, 1, 7, 1, False), [(2 - first, 2), (4, 2)])
        swap(0, first, 2).wait_recv()
        for a in inside[:2]:
            owner(a)
        offer(1, 2 - first, 2)
        total[7] = add(acc, [(6, 1)])
        offer(2, 4, 4)
        swap(1, 2 - first, 2).wait_recv()
        for a in inside[2:]:
            owner(a)
        swap(2, 4, 4).wait_recv()
        for a in range(4, 8):
            owner(a)
        swap(0, first, 2).wait_send()
        swap(1, 2 - first, 2).wait_send()
        swap(2, 4, 4).wait_send()

    @pl.when(upper == 1)
    def _():
        acc = add(jnp.zeros((block, dom), F32), [(4, 2)])
        offer(0, 4, 2)
        acc = add(acc + product(7, 1, 7, 1, False), [(6, 1), (0, 2)])
        swap(0, 4, 2).wait_recv()
        owner(4 + y)
        total[7] = add(acc, [(2, 2)])
        offer(1, 6, 2)
        offer(2, 0, 4)
        owner(5 - y)
        swap(1, 6, 2).wait_recv()
        for a in (6, 7):
            owner(a)
        swap(2, 0, 4).wait_recv()
        for a in inside:
            owner(a)
        swap(0, 4, 2).wait_send()
        swap(1, 6, 2).wait_send()
        swap(2, 0, 4).wait_send()

    acc = total[0, mine] + xrecv[0].astype(F32)
    for a in range(1, n):
        remote(rsend.at[a], rrecv.at[a], rs_sem.at[a], rr_sem.at[a], tok=at(1)).wait_recv()
        acc = acc + rrecv[a].astype(F32)
    out[...] = acc
    for a in range(1, n):
        give(a).wait_send()
    for copy in copies:
        copy.wait_send()


def on_device_near_far(acts, grads, losses, sources):
    block, lh, width = acts.shape
    dom = losses.shape[1]
    n = lax.axis_size("tok")
    layers = lh * lax.axis_size("lay")
    scale = 1.0 / math.sqrt(n * block * layers)
    half = block // 2
    dma = pltpu.SemaphoreType.DMA
    pairs = n * block * block * lh
    return pl.pallas_call(
        functools.partial(near_far, scale),
        out_shape=pltpu.VMEM((half, dom), F32),
        in_specs=[pl.BlockSpec(memory_space=pl.ANY)] * 4,
        out_specs=pl.BlockSpec(memory_space=pltpu.VMEM),
        scratch_shapes=[
            pltpu.VMEM((2, block, lh, width), BF16),
            pltpu.VMEM((2, block * lh, width), F32),
            pltpu.VMEM((n, 2 * block + half + 16, width), BF16),
            pltpu.VMEM((n, 2 * block + half + 16, width), BF16),
            pltpu.VMEM((1, block), jnp.int32),
            pltpu.VMEM((n, block, dom), BF16),
            pltpu.VMEM((n, 1, block), F32),
            pltpu.VMEM((n, block, 128), F32),
            pltpu.VMEM((n, block, dom), F32),
            pltpu.VMEM((n, half, dom), BF16),
            pltpu.VMEM((n, half, dom), BF16),
            pltpu.VMEM((n, half, dom), BF16),
            pltpu.VMEM((n, half, dom), BF16),
            dma((n,)), dma((n,)), dma((4,)), dma((n,)), dma((3,)), dma((3,)),
            dma((n,)), dma((n,)), dma((n,)), dma((n,)), dma((4,)),
        ],
        compiler_params=pltpu.CompilerParams(
            collective_id=1, has_side_effects=True, vmem_limit_bytes=56 * 1024 * 1024
        ),
        cost_estimate=pl.CostEstimate(
            flops=2 * pairs * (2 * width + dom), bytes_accessed=4 * block * lh * width, transcendentals=0
        ),
    )(acts, grads, losses, sources.reshape(1, block)) * scale


def solution(mesh):
    placed = (
        P(("grp", "tok"), "lay", None),
        P(("grp", "tok"), "lay", None),
        P(("grp", "tok"), None),
        P(("grp", "tok")),
    )
    def part(acts, grads, losses, sources):
        paired = acts.shape[1] == mesh.shape["tok"] == 8
        return (on_device_near_far if paired else on_device)(acts, grads, losses, sources)

    return jax.shard_map(
        part,
        mesh=mesh,
        in_specs=placed,
        out_specs=P(("grp", "tok", "lay"), None),
        check_vma=False,
    )
```
